512 devices in a mesh: cell: 2 (over core), grp: 256 (over z, y, x).
Axes of the slice: x: 4, y: 8, z: 8, core: 2. Of those that a mesh axis runs over, the one named last changes fastest.
Arguments:
- v_free: float32 [3, 4194304], P(None, 'grp'), may hold values from -6 to 6
- inv_mass: float32 [4194304], P('grp'), may hold values from 0.2 to 5
- pairs: int32 [2, 16384, 128], P(None, ('cell', 'grp')), may hold values from 0 to 20479, as said below
- angles: float32 [2, 16384, 128], P(None, ('cell', 'grp')), may hold values from -3.140625 to 3.140625
- bias: float32 [16384, 128], P(('cell', 'grp')), may hold values from -6 to 6
- friction: float32 [16384, 128], P(('cell', 'grp')), may hold values from 0.2 to 1
- counts: int32 [16384], P(('cell', 'grp')), may hold values from 16 to 128, as said below
Outputs:
- velocity: float32 [3, 4194304], P(None, 'grp')
- impulses: float32 [3, 16384, 128], P(None, ('cell', 'grp'))
The draws below stay inside these ranges and needn't reach their ends.
Inputs may be any that keep to these rules, and one draw needn't show every extreme that they name: A spatial cell's window of bodies holds the last 2048 bodies of the previous cell (positions 0 to 2047), the cell's own 16384 bodies (positions 2048 to 18431) and the first 2048 bodies of the next cell (the remaining positions). pairs[0] is always one of the cell's own bodies; pairs[1] is another own body or a rim body of a neighbouring cell. No slot of the first cell names the previous rim and no slot of the last cell names the next rim. `counts`: the first block of each 32 blocks is full.
All inputs are finite; a program needn't handle non-finite values.
Results may differ from the reference program's by a relative error of at most 0.0001.
Values sent between devices are 32-bit elements; how exact they have to be, the bound alone decides.
No kernel may reach another device: no remote copies, remote signals or barrier semaphores. Data moves between devices by JAX's collectives and lax.ppermute only.
A program may use at most 128 MiB of HBM per device.

```python
import math
import jax
import jax.numpy as jnp
from jax import lax

B_DEV = 16384
RIM = 2048
BLK_DEV = 32
CONTACTS = 128
ITERS = 3
CELLS = 256
NB = 4194304
NBLK = 16384


def draw_pairs(key, part):
    rows = jnp.arange(NBLK, dtype=jnp.int32)[:, None] + jnp.zeros((1, CONTACTS), jnp.int32)
    columns = jnp.arange(CONTACTS, dtype=jnp.int32)[None, :] + jnp.zeros((NBLK, 1), jnp.int32)
    cell_index = rows // BLK_DEV % CELLS
    last_cell = CELLS - 1
    keys = jax.random.split(key, 4)
    kind = jax.random.randint(keys[0], (NBLK, CONTACTS), 0, 4)
    kind = jnp.where((kind == 0) & (cell_index == 0), 2, kind)
    kind = jnp.where((kind == 1) & (cell_index == last_cell), 3, kind)
    at_low = (rows == BLK_DEV) & (columns == 0)
    at_high = (rows == 0) & (columns == 0)
    kind = jnp.where(at_low, 0, jnp.where(at_high, 1, kind))
    local_a = jax.random.randint(keys[1], (NBLK, CONTACTS), 0, B_DEV)
    rim_pick = jax.random.randint(keys[2], (NBLK, CONTACTS), 0, RIM)
    rim_pick = jnp.where(at_low, 0, jnp.where(at_high, RIM - 1, rim_pick))
    other = jax.random.randint(keys[3], (NBLK, CONTACTS), 1, B_DEV)
    first_local = jnp.where(kind == 0, local_a % RIM, jnp.where(kind == 1, B_DEV - 1 - local_a % RIM, local_a))
    second = jnp.where(kind == 0, rim_pick, jnp.where(kind == 1, RIM + B_DEV + rim_pick, RIM + (local_a + other) % B_DEV))
    first = RIM + first_local
    return jnp.stack([first, second]).astype(jnp.int32)


def draw_counts(key, part):
    rows = jnp.arange(NBLK, dtype=jnp.int32)
    cell_index = rows // BLK_DEV % CELLS
    lowest = jnp.where(cell_index % 3 == 0, 96, 16)
    drawn = jax.random.randint(key, (NBLK,), lowest, CONTACTS + 1)
    drawn = jnp.where((rows % BLK_DEV == 1) & (cell_index % 3 != 0), 16, drawn)
    return jnp.where(rows % BLK_DEV == 0, CONTACTS, drawn).astype(jnp.int32)


def steps_of(stream_key, extent, shards, least, largest):
    def one(axis_at, blocks):
        steps = jax.random.uniform(jax.random.fold_in(jax.random.fold_in(stream_key, 6), axis_at), (blocks,), jnp.float32, least / len(shards), largest / len(shards))
        return jnp.repeat(jnp.exp(steps), extent[axis_at] // blocks).reshape((-1,) + (1,) * (len(extent) - axis_at - 1))

    loudness = one(*shards[0])
    for cut in shards[1:]:
        loudness = loudness * one(*cut)
    return loudness


def bell_draw(stream_key, extent, scale, bound, cuts=(), kind=jnp.bfloat16):
    result = jax.random.normal(stream_key, extent, jnp.float32) * scale
    if len(cuts) > 0:
        result = steps_of(stream_key, extent, cuts, -0.22, 0.18) * result
    return jnp.clip(result, min=-bound, max=bound).astype(kind)


def setup_inputs(seed: int = 0) -> dict:
    arg_keys = jax.random.split(jax.random.key(seed), 8)
    return {
        "v_free": bell_draw(arg_keys[0], (3, NB), 1.0, 6.0, ((1, 256),), jnp.float32),
        "inv_mass": jnp.clip(jnp.exp(math.log(5.0) - 3.218876 * jax.random.uniform(arg_keys[1], (NB,), jnp.float32) ** steps_of(arg_keys[1], (NB,), ((0, 256),), -0.2, 0.2)), 0.2, 5.0),
        "pairs": draw_pairs(jax.random.fold_in(arg_keys[7], 71), 0),
        "angles": jnp.clip(jax.random.uniform(arg_keys[3], (2, NBLK, CONTACTS), jnp.float32, -3.140625, 3.140625), -3.140625, 3.140625),
        "bias": bell_draw(arg_keys[4], (NBLK, CONTACTS), 1.0, 6.0, ((0, 512),), jnp.float32),
        "friction": jnp.clip(0.2 + 0.8 * jax.random.uniform(arg_keys[5], (NBLK, CONTACTS), jnp.float32) ** steps_of(arg_keys[5], (NBLK, CONTACTS), ((0, 512),), -0.2, 0.2), 0.2, 1.0),
        "counts": draw_counts(jax.random.fold_in(arg_keys[7], 71), 0),
    }


relax_factor = 0.6
tangent_floor = 0.05

def frames(angles):
    sin_polar = jnp.sin(angles[0])
    cos_polar = jnp.cos(angles[0])
    sin_azim = jnp.sin(angles[1])
    cos_azim = jnp.cos(angles[1])
    normal = jnp.stack([sin_polar * cos_azim, sin_polar * sin_azim, cos_polar])
    first_tan = jnp.stack([cos_polar * cos_azim, cos_polar * sin_azim, -sin_polar])
    second_tan = jnp.stack([-sin_azim, cos_azim, jnp.zeros_like(sin_azim)])
    return (normal, first_tan, second_tan)

def contact_update(relative, lambdas, normal, first_tan, second_tan, reduced, bias, friction, active):
    speed_n = lax.optimization_barrier(jnp.sum(normal * relative, axis=0)) + bias
    speed_a = lax.optimization_barrier(jnp.sum(first_tan * relative, axis=0))
    speed_b = lax.optimization_barrier(jnp.sum(second_tan * relative, axis=0))
    trial_n = lambdas[0] - relax_factor * reduced * speed_n
    trial_a = lambdas[1] - relax_factor * reduced * speed_a
    trial_b = lambdas[2] - relax_factor * reduced * speed_b
    normal_imp = jnp.maximum(trial_n, 0.0)
    tan_size = jnp.sqrt(trial_a * trial_a + trial_b * trial_b)
    factor = jnp.minimum(1.0, friction * normal_imp / jnp.maximum(tan_size, tangent_floor))
    fresh = jnp.stack([normal_imp, trial_a * factor, trial_b * factor]) * active[None]
    force = normal * fresh[0] + first_tan * fresh[1] + second_tan * fresh[2]
    return (fresh, force)

def reference(v_free, inv_mass, pairs, angles, bias, friction, counts):
    block_rows = jnp.arange(bias.shape[0], dtype=jnp.int32)
    cell_of = block_rows // BLK_DEV % CELLS
    offset = (cell_of * B_DEV - RIM).astype(jnp.int32)[:, None]
    first = (pairs[0] + offset).astype(jnp.int32)
    second = (pairs[1] + offset).astype(jnp.int32)
    slots = jnp.arange(bias.shape[1], dtype=jnp.int32)
    active = (slots[None, :] < counts[:, None]).astype(jnp.float32)
    normal, first_tan, second_tan = frames(angles)
    reduced = 1.0 / (inv_mass[first] + inv_mass[second])
    lambdas = jnp.zeros((3,) + bias.shape, jnp.float32)
    velocity = v_free
    for sweep in range(ITERS):
        relative = velocity[:, first] - velocity[:, second]
        lambdas, force = contact_update(relative, lambdas, normal, first_tan, second_tan, reduced, bias, friction, active)
        total = jnp.zeros_like(v_free).at[:, first].add(force).at[:, second].add(-force)
        velocity = v_free + inv_mass[None, :] * total
    return (velocity, lambdas)
```

```python
import jax
import jax.numpy as jnp
from jax import lax
from jax.experimental import pallas as pl
from jax.experimental.pallas import tpu as pltpu
from jax.sharding import PartitionSpec as P

RIM = 2048
ITERS = 3
LANES = 128
relax_factor = 0.6
tangent_floor = 0.05

f32 = jnp.float32
bf16 = jnp.bfloat16


def call(body, out_shapes, *args, specs=None, scratch=()):
    kw = {} if specs is None else {"in_specs": specs}
    return pl.pallas_call(
        body,
        out_shape=[jax.ShapeDtypeStruct(s, f32) for s in out_shapes],
        scratch_shapes=list(scratch),
        **kw,
    )(*args)


def gather_rows(table, comps, start, rows, base, positions, sums):
    his = [p // LANES for p in positions]
    los = [p % LANES for p in positions]

    def group(g, sums):
        sums = [list(s) for s in sums]
        first = pl.multiple_of(start + g * 8, 8)
        for j in range(8):
            hits = [hi == first + (base + j) for hi in his]
            for c in range(comps):
                row = jnp.broadcast_to(table[c, pl.ds(first + j, 1), :], los[0].shape)
                for k, lo in enumerate(los):
                    got = jnp.take_along_axis(row, lo, axis=1, mode="promise_in_bounds")
                    sums[k][c] = jnp.where(hits[k], got, sums[k][c])
        return tuple(tuple(s) for s in sums)

    init = tuple(tuple(s) for s in sums)
    return lax.fori_loop(0, rows // 8, group, init)


def update(lam, rel, trig, scaled, bias, friction, active):
    sp, cp, sq, cq = trig
    n = (sp * cq, sp * sq, cp)
    a = (cp * cq, cp * sq, -sp)
    b = (-sq, cq)
    un = (n[0] * rel[0] + n[1] * rel[1] + n[2] * rel[2]) + bias
    ua = a[0] * rel[0] + a[1] * rel[1] + a[2] * rel[2]
    ub = b[0] * rel[0] + b[1] * rel[1]
    yn = lam[0] - scaled * un
    ya = lam[1] - scaled * ua
    yb = lam[2] - scaled * ub
    top = jnp.maximum(yn, 0.0)
    size = jnp.sqrt(ya * ya + yb * yb)
    factor = jnp.minimum(1.0, friction * top / jnp.maximum(size, tangent_floor))
    fn = active * top
    fa = active * (factor * ya)
    fb = active * (factor * yb)
    force = (
        n[0] * fn + a[0] * fa + b[0] * fb,
        n[1] * fn + a[1] * fa + b[1] * fb,
        n[2] * fn + a[2] * fa,
    )
    return (fn, fa, fb), force


def scatter(pairs, force, lhs, rhs, stage, out, rows):
    half = rows // 2
    blocks = pairs.shape[1]
    for c in range(3):
        high = force[c].astype(bf16).astype(f32)
        stage[2 * c] = high
        stage[2 * c + 1] = force[c] - high
    row_ids = lax.broadcasted_iota(jnp.int32, (half, LANES), 0).astype(f32).astype(bf16)
    col_ids = lax.broadcasted_iota(jnp.int32, (2 * LANES, LANES), 0).astype(f32).astype(bf16)
    for side in range(2):
        pos = pairs[side]
        hi = pos // LANES
        upper = (hi >= half).astype(jnp.int32)
        stage[6 + 2 * side] = (hi - half * upper).astype(f32)
        stage[7 + 2 * side] = (pos % LANES + LANES * upper).astype(f32)
    one = jnp.ones((), bf16)
    zero = jnp.zeros((), bf16)

    def wide(k, b, n):
        return jnp.broadcast_to(stage[k, pl.ds(b, 1), :], (n, LANES)).astype(bf16)

    for b in range(blocks):
        vals = [wide(k, b, half) for k in range(6)]
        for side in range(2):
            at = pl.ds((2 * b + side) * LANES, LANES)
            hit = wide(6 + 2 * side, b, half) == row_ids
            for k in range(6):
                lhs[pl.ds(k * half, half), at] = jnp.where(hit, vals[k], zero)
            col = wide(7 + 2 * side, b, 2 * LANES) == col_ids
            rhs[:, at] = jnp.where(col, one if side == 0 else -one, zero)
    prod = lax.dot_general(
        lhs[...], rhs[...], (((1,), (1,)), ((), ())), preferred_element_type=f32
    )
    for c in range(3):
        both = prod[2 * c * half : (2 * c + 1) * half] + prod[(2 * c + 1) * half : (2 * c + 2) * half]
        out[c, :half, :] = both[:, :LANES]
        out[c, half:, :] = both[:, LANES:]


def scatter_scratch(rows, blocks):
    deep = 2 * blocks * LANES
    return (
        pltpu.VMEM((3 * rows, deep), bf16),
        pltpu.VMEM((2 * LANES, deep), bf16),
        pltpu.VMEM((10, blocks, LANES), f32),
    )


def on_device(v_free, inv_mass, pairs, angles, bias, friction, counts):
    width = v_free.shape[1]
    own = width // LANES
    rim = RIM // LANES
    rows = own + 2 * rim
    blocks = bias.shape[0]
    slots = (blocks, LANES)
    count = lax.axis_size("grp")
    up = [(i, i + 1) for i in range(count - 1)]
    down = [(i + 1, i) for i in range(count - 1)]
    partner = [(0, 1), (1, 0)]

    def to_both(low, high):
        return lax.ppermute(high, "grp", up), lax.ppermute(low, "grp", down)

    mass2 = inv_mass.reshape(own, LANES)
    stacked = jnp.concatenate([v_free, inv_mass[None, :]], axis=0)
    from_prev, from_next = to_both(stacked[:, :RIM], stacked[:, width - RIM :])

    def prepare(v_ref, mass_ref, pairs_ref, angles_ref, counts_ref, vf, part, trig, act):
        for r in range(own):
            for c in range(3):
                vf[c, r : r + 1, :] = v_ref[c : c + 1, r * LANES : (r + 1) * LANES]
        vf[3] = mass_ref[...]
        for i in range(2):
            trig[2 * i] = jnp.sin(angles_ref[i])
            trig[2 * i + 1] = jnp.cos(angles_ref[i])
        lane = lax.broadcasted_iota(jnp.int32, (1, LANES), 1)
        for b in range(blocks):
            act[b : b + 1, :] = jnp.where(lane < counts_ref[b], 1.0, 0.0)
        zero = jnp.zeros((8, LANES), f32)
        for k in range(blocks // 8):
            at = slice(8 * k, 8 * k + 8)
            one, two = gather_rows(
                vf, 4, 0, own, rim, [pairs_ref[0, at, :], pairs_ref[1, at, :]], [[zero] * 4, [zero] * 4]
            )
            for c in range(4):
                part[c, at, :] = one[c]
                part[4 + c, at, :] = two[c]

    vmem = pl.BlockSpec(memory_space=pltpu.VMEM)
    smem = pl.BlockSpec(memory_space=pltpu.SMEM)
    vf, part, trig, act = call(
        prepare,
        [(4, own, LANES), (8,) + slots, (4,) + slots, slots],
        v_free, mass2, pairs, angles, counts,
        specs=[vmem] * 4 + [smem],
    )

    def first_sweep(part_ref, prev_ref, next_ref, pairs_ref, trig_ref, act_ref, bias_ref, fric_ref,
                    rims, scaled_ref, lam_ref, total, lhs, rhs, stage):
        for r in range(rim):
            for c in range(4):
                at = slice(r * LANES, (r + 1) * LANES)
                rims[c, r : r + 1, :] = prev_ref[c : c + 1, at]
                rims[c, rim + r : rim + r + 1, :] = next_ref[c : c + 1, at]
        two = [part_ref[4 + c] for c in range(4)]
        pos = pairs_ref[1]
        (two,) = gather_rows(rims, 4, 0, rim, 0, [pos], [two])
        (two,) = gather_rows(rims, 4, rim, rim, own, [pos], [two])
        rel = [part_ref[c] - two[c] for c in range(3)]
        scaled = relax_factor * (1.0 / (part_ref[3] + two[3]))
        scaled_ref[...] = scaled
        zero = jnp.zeros(slots, f32)
        fresh, force = update(
            (zero, zero, zero), rel, [trig_ref[k] for k in range(4)], scaled, bias_ref[...], fric_ref[...], act_ref[...]
        )
        for c in range(3):
            lam_ref[c] = fresh[c]
        scatter(pairs_ref, force, lhs, rhs, stage, total, rows)

    rims, scaled, lam, total = call(
        first_sweep,
        [(4, 2 * rim, LANES), slots, (3,) + slots, (3, rows, LANES)],
        part, from_prev, from_next, pairs, trig, act, bias, friction,
        scratch=scatter_scratch(rows, blocks),
    )

    for sweep in range(1, ITERS):
        other = lax.ppermute(total, "cell", partner)
        edge_low = total[:, : 2 * rim] + other[:, : 2 * rim]
        edge_high = total[:, own:] + other[:, own:]
        got_prev, got_next = to_both(edge_low, edge_high)

        def inner(total_ref, other_ref, vf_ref, pairs_ref, part, vel):
            for c in range(3):
                vel[c] = vf_ref[c, rim : own - rim] + vf_ref[3, rim : own - rim] * (
                    total_ref[c, 2 * rim : own] + other_ref[c, 2 * rim : own]
                )
            zero = jnp.zeros((8, LANES), f32)
            for k in range(blocks // 8):
                at = slice(8 * k, 8 * k + 8)
                one, two = gather_rows(
                    vel, 3, 0, own - 2 * rim, 2 * rim,
                    [pairs_ref[0, at, :], pairs_ref[1, at, :]], [[zero] * 3, [zero] * 3],
                )
                for c in range(3):
                    part[c, at, :] = one[c]
                    part[3 + c, at, :] = two[c]

        (part,) = call(
            inner, [(6,) + slots], total, other, vf, pairs,
            scratch=[pltpu.VMEM((3, own - 2 * rim, LANES), f32)],
        )

        def outer(part_ref, low_ref, high_ref, prev_ref, next_ref, vf_ref, rims_ref, pairs_ref, trig_ref, act_ref,
                  bias_ref, fric_ref, scaled_ref, old_ref, lam_ref, total, vel, lhs, rhs, stage):
            for c in range(3):
                low = low_ref[c] + prev_ref[c]
                high = high_ref[c] + next_ref[c]
                vel[c, :rim] = rims_ref[c, :rim] + rims_ref[3, :rim] * low[:rim]
                vel[c, rim : 2 * rim] = vf_ref[c, :rim] + vf_ref[3, :rim] * low[rim:]
                vel[c, 2 * rim : 3 * rim] = vf_ref[c, own - rim :] + vf_ref[3, own - rim :] * high[:rim]
                vel[c, 3 * rim :] = rims_ref[c, rim:] + rims_ref[3, rim:] * high[rim:]
            for k in range(blocks // 8):
                at = slice(8 * k, 8 * k + 8)
                sums = [[part_ref[c, at, :] for c in range(3)], [part_ref[3 + c, at, :] for c in range(3)]]
                both = [pairs_ref[0, at, :], pairs_ref[1, at, :]]
                sums = gather_rows(vel, 3, 0, 2 * rim, 0, both, sums)
                one, two = gather_rows(vel, 3, 2 * rim, 2 * rim, own - 2 * rim, both, sums)
                rel = [one[c] - two[c] for c in range(3)]
                fresh, force = update(
                    [old_ref[c, at, :] for c in range(3)], rel, [trig_ref[i, at, :] for i in range(4)],
                    scaled_ref[at, :], bias_ref[at, :], fric_ref[at, :], act_ref[at, :],
                )
                for c in range(3):
                    lam_ref[c, at, :] = fresh[c]
                    stage[c, at, :] = force[c]
            scatter(pairs_ref, [stage[c] for c in range(3)], lhs, rhs, stage, total, rows)

        lam, total = call(
            outer,
            [(3,) + slots, (3, rows, LANES)],
            part, edge_low, edge_high, got_prev, got_next, vf, rims, pairs, trig, act, bias, friction, scaled, lam,
            scratch=(pltpu.VMEM((3, 4 * rim, LANES), f32),) + scatter_scratch(rows, blocks),
        )

    other = lax.ppermute(total, "cell", partner)
    low = total[:, : 2 * rim] + other[:, : 2 * rim]
    high = total[:, own:] + other[:, own:]
    got_prev, got_next = to_both(low[:, :rim], high[:, rim:])

    def finish(total_ref, other_ref, prev_ref, next_ref, vf_ref, out):
        for c in range(3):
            t = total_ref[c, rim : rim + own] + other_ref[c, rim : rim + own]
            head = t[:rim] + prev_ref[c]
            tail = t[own - rim :] + next_ref[c]
            v = vf_ref[c] + vf_ref[3] * jnp.concatenate([head, t[rim : own - rim], tail], axis=0)
            for r in range(own):
                out[c : c + 1, r * LANES : (r + 1) * LANES] = v[r : r + 1]

    (velocity,) = call(finish, [(3, width)], total, other, got_prev, got_next, vf)
    return (velocity, lam)


def solution(mesh):
    return jax.shard_map(
        on_device,
        mesh=mesh,
        in_specs=(
            P(None, "grp"),
            P("grp"),
            P(None, ("cell", "grp"), None),
            P(None, ("cell", "grp"), None),
            P(("cell", "grp"), None),
            P(("cell", "grp"), None),
            P(("cell", "grp")),
        ),
        out_specs=(P(None, "grp"), P(None, ("cell", "grp"), None)),
        check_vma=False,
    )
```

```python
import jax
import jax.numpy as jnp
from jax import lax
from jax.experimental import pallas as pl
from jax.experimental.pallas import tpu as pltpu
from jax.sharding import PartitionSpec as P

RIM = 2048
ITERS = 3
LANES = 128
relax_factor = 0.6
tangent_floor = 0.05

f32 = jnp.float32
bf16 = jnp.bfloat16
VM = pl.BlockSpec(memory_space=pltpu.VMEM)
SM = pl.BlockSpec(memory_space=pltpu.SMEM)
HB = pl.BlockSpec(memory_space=pltpu.HBM)


def call(body, out_shapes, *args, specs=None, scratch=(), onchip=None):
    specs = [VM] * len(args) if specs is None else specs
    args = [x if s is SM else pltpu.with_memory_space_constraint(x, pltpu.HBM if s is HB else pltpu.VMEM) for x, s in zip(args, specs)]
    shapes = [s if isinstance(s, tuple) and len(s) == 2 and isinstance(s[0], tuple) else (s, f32) for s in out_shapes]
    keep = [True] * len(shapes) if onchip is None else onchip
    return pl.pallas_call(
        body,
        out_shape=[pltpu.VMEM(s, t) if k else jax.ShapeDtypeStruct(s, t) for (s, t), k in zip(shapes, keep)],
        in_specs=specs,
        out_specs=[VM] * len(shapes),
        scratch_shapes=list(scratch),
        compiler_params=pltpu.CompilerParams(vmem_limit_bytes=24 << 20),
    )(*args)


def split(positions):
    return lax.shift_right_logical(positions, 7), positions & (LANES - 1)


def lane_gather(row, lo):
    dims = lax.GatherDimensionNumbers(
        offset_dims=(), collapsed_slice_dims=(1,), start_index_map=(1,),
        operand_batching_dims=(0,), start_indices_batching_dims=(0,),
    )
    return lax.gather(row, lo[:, :, None], dims, (1, 1), mode=lax.GatherScatterMode.PROMISE_IN_BOUNDS)


def gather_rows(table, comps, start, rows, base, his, los, sums):
    sums = [list(s) for s in sums]
    for r in range(start, start + rows):
        hits = [hi == base + r for hi in his]
        for c in range(comps):
            row = jnp.broadcast_to(table[c, r : r + 1, :], los[0].shape)
            for k, lo in enumerate(los):
                sums[k][c] = jnp.where(hits[k], lane_gather(row, lo), sums[k][c])
    return sums


def update(lam, rel, trig, scaled, bias, friction, active):
    sp, cp, sq, cq = trig
    n = (sp * cq, sp * sq, cp)
    a = (cp * cq, cp * sq, -sp)
    b = (-sq, cq)
    un = (n[0] * rel[0] + n[1] * rel[1] + n[2] * rel[2]) + bias
    ua = a[0] * rel[0] + a[1] * rel[1] + a[2] * rel[2]
    ub = b[0] * rel[0] + b[1] * rel[1]
    yn = lam[0] - scaled * un
    ya = lam[1] - scaled * ua
    yb = lam[2] - scaled * ub
    top = jnp.maximum(yn, 0.0)
    size = jnp.sqrt(ya * ya + yb * yb)
    factor = jnp.minimum(1.0, friction * top / jnp.maximum(size, tangent_floor))
    fn = active * top
    fa = active * (factor * ya)
    fb = active * (factor * yb)
    force = (
        n[0] * fn + a[0] * fa + b[0] * fb,
        n[1] * fn + a[1] * fa + b[1] * fb,
        n[2] * fn + a[2] * fa,
    )
    return (fn, fa, fb), force


def wide(ref, b, n):
    return jnp.broadcast_to(ref[pl.ds(b, 1), :], (n, LANES)).astype(bf16)


def spots(pos, half):
    hi, lo = split(pos)
    upper = (hi >= half).astype(jnp.int32)
    return (hi - half * upper).astype(f32), (lo + LANES * upper).astype(f32)


def build_columns(first, count, cols, rhs):
    ids = lax.broadcasted_iota(jnp.int32, (2 * LANES, LANES), 0).astype(f32).astype(bf16)
    zero = jnp.zeros((), bf16)
    for i in range(count):
        for side in range(2):
            sign = jnp.full((), 1 - 2 * side, bf16)
            at = pl.multiple_of((2 * (first + i) + side) * LANES, LANES)
            rhs[:, pl.ds(at, LANES)] = jnp.where(wide(cols.at[side], first + i, 2 * LANES) == ids, sign, zero)


def scatter_group(first, count, force, stage, rowsel, rhs, lhs, half):
    for c in range(3):
        high = force[c].astype(bf16).astype(f32)
        stage[2 * c, first : first + count] = high
        stage[2 * c + 1, first : first + count] = force[c] - high
    ids = lax.broadcasted_iota(jnp.int32, (half, LANES), 0).astype(f32).astype(bf16)
    zero = jnp.zeros((), bf16)
    for b in range(first, first + count):
        vals = [wide(stage.at[k], b, half) for k in range(6)]
        for side in range(2):
            at = (2 * b + side) * LANES
            hit = wide(rowsel.at[side], b, half) == ids
            for k in range(6):
                lhs[k * half : (k + 1) * half, at : at + LANES] = jnp.where(hit, vals[k], zero)
    deep = slice(2 * first * LANES, 2 * (first + count) * LANES)
    return lax.dot_general(lhs[:, deep], rhs[:, deep], (((1,), (1,)), ((), ())), preferred_element_type=f32)


def write_total(prod, total, half):
    for c in range(3):
        both = prod[2 * c * half : (2 * c + 1) * half] + prod[(2 * c + 1) * half : (2 * c + 2) * half]
        total[c, :half, :] = both[:, :LANES]
        total[c, half:, :] = both[:, LANES:]


def on_device(v_free, inv_mass, pairs, angles, bias, friction, counts):
    width = v_free.shape[1]
    own = width // LANES
    rim = RIM // LANES
    rows = own + 2 * rim
    half = rows // 2
    blocks = bias.shape[0]
    slots = (blocks, LANES)
    deep = 2 * blocks * LANES
    group = 8
    count = lax.axis_size("grp")
    core = lax.axis_index("cell").astype(jnp.int32).reshape(1)
    steps = [(i, i + 1) for i in range(count - 1)] + [(count + i + 1, count + i) for i in range(count - 1)]

    def around(mine):
        return lax.all_gather(lax.ppermute(mine, ("cell", "grp"), steps), "cell")

    def load(v_hbm, mass_hbm, counts_hbm, pairs_hbm, angles_hbm, bias_hbm, fric_hbm, core_ref,
             vf, mine, act, pairs_ref, angles_ref, bias_ref, fric_ref, v_ref, counts_ref, sems):
        pairs_of = [(v_hbm, v_ref), (mass_hbm, vf.at[3]), (counts_hbm, counts_ref), (pairs_hbm, pairs_ref), (angles_hbm, angles_ref),
                    (bias_hbm, bias_ref), (fric_hbm, fric_ref)]
        copies = [pltpu.make_async_copy(src, dst, sems.at[i]) for i, (src, dst) in enumerate(pairs_of)]
        for copy in copies:
            copy.start()
        copies[0].wait()
        for r in range(own):
            for c in range(3):
                vf[c, r : r + 1, :] = v_ref[c : c + 1, r * LANES : (r + 1) * LANES]
        copies[1].wait()
        upward = core_ref[0] == 0
        for c in range(4):
            mine[c] = jnp.where(upward, vf[c, own - rim :], vf[c, :rim])
        copies[2].wait()
        lane = lax.broadcasted_iota(jnp.int32, (1, LANES), 1)
        for b in range(blocks):
            act[b : b + 1, :] = jnp.where(lane < counts_ref[b], 1.0, 0.0)
        for copy in copies[3:]:
            copy.wait()

    vf, mine, act, pairs, angles, bias, friction = call(
        load,
        [(4, own, LANES), (4, rim, LANES), slots, (pairs.shape, jnp.int32), angles.shape, slots, slots],
        v_free, inv_mass.reshape(own, LANES), counts, pairs, angles, bias, friction, core,
        specs=[HB] * 7 + [SM],
        scratch=[pltpu.VMEM((3, width), f32), pltpu.SMEM((blocks,), jnp.int32), pltpu.SemaphoreType.DMA((7,))],
    )
    got_rims = around(mine)

    def prepare(vf, pairs_ref, angles_ref, part, trig, rowsel, rhs, cols):
        for i in range(2):
            rowsel[i], cols[i] = spots(pairs_ref[i], half)
        zero = jnp.zeros((group, LANES), f32)

        def some(k, carry):
            first = pl.multiple_of(k * group, group)
            at = pl.ds(first, group)
            build_columns(first, group, cols, rhs)
            for i in range(2):
                trig[2 * i, at, :] = jnp.sin(angles_ref[i, at, :])
                trig[2 * i + 1, at, :] = jnp.cos(angles_ref[i, at, :])
            his, los = zip(*(split(pairs_ref[i, at, :]) for i in range(2)))
            one, two = gather_rows(vf, 4, 0, own, rim, his, los, [[zero] * 4, [zero] * 4])
            for c in range(4):
                part[c, at, :] = one[c]
                part[4 + c, at, :] = two[c]
            return carry

        lax.fori_loop(0, blocks // group, some, 0)

    part, trig, rowsel, rhs = call(
        prepare,
        [(8,) + slots, (4,) + slots, (2,) + slots, ((2 * LANES, deep), bf16)],
        vf, pairs, angles,
        scratch=[pltpu.VMEM((2,) + slots, f32)],
    )

    def first_sweep(part_ref, got_ref, pairs_ref, trig_ref, act_ref, bias_ref, fric_ref, rowsel_ref, rhs_ref,
                    rims, scaled_ref, lam_ref, total, lhs, stage):
        for c in range(4):
            rims[c, :rim] = got_ref[0, c]
            rims[c, rim:] = got_ref[1, c]
        zero = jnp.zeros((group, LANES), f32)
        prod = None
        for k in range(blocks // group):
            at = slice(group * k, group * (k + 1))
            hi, lo = split(pairs_ref[1, at, :])
            two = [[part_ref[4 + c, at, :] for c in range(4)]]
            two = gather_rows(rims, 4, 0, rim, 0, [hi], [lo], two)
            (two,) = gather_rows(rims, 4, rim, rim, own, [hi], [lo], two)
            rel = [part_ref[c, at, :] - two[c] for c in range(3)]
            scaled = relax_factor * (1.0 / (part_ref[3, at, :] + two[3]))
            scaled_ref[at, :] = scaled
            fresh, force = update(
                (zero, zero, zero), rel, [trig_ref[i, at, :] for i in range(4)],
                scaled, bias_ref[at, :], fric_ref[at, :], act_ref[at, :],
            )
            for c in range(3):
                lam_ref[c, at, :] = fresh[c]
            more = scatter_group(group * k, group, force, stage, rowsel_ref, rhs_ref, lhs, half)
            prod = more if prod is None else prod + more
        write_total(prod, total, half)

    scatter_scratch = [pltpu.VMEM((6 * half, deep), bf16), pltpu.VMEM((6,) + slots, f32)]
    rims, scaled, lam, total = call(
        first_sweep,
        [(4, 2 * rim, LANES), slots, (3,) + slots, (3, rows, LANES)],
        part, got_rims, pairs, trig, act, bias, friction, rowsel, rhs,
        scratch=scatter_scratch,
    )

    def edges(wide_rows):
        def body(both_ref, core_ref, mine, *kept):
            upward = core_ref[0] == 0
            for c in range(3):
                below = both_ref[0, c, :wide_rows] + both_ref[1, c, :wide_rows]
                above = both_ref[0, c, rows - wide_rows :] + both_ref[1, c, rows - wide_rows :]
                mine[c] = jnp.where(upward, above, below)
                if kept:
                    kept[0][c] = below
                    kept[1][c] = above

        return body

    for sweep in range(1, ITERS):
        both = lax.all_gather(total, "cell")
        mine, low, high = call(edges(2 * rim), [(3, 2 * rim, LANES)] * 3, both, core, specs=[VM, SM])
        got = around(mine)

        def inner(both_ref, vf_ref, pairs_ref, part, vel):
            for c in range(3):
                vel[c] = vf_ref[c, rim : own - rim] + vf_ref[3, rim : own - rim] * (
                    both_ref[0, c, 2 * rim : own] + both_ref[1, c, 2 * rim : own]
                )
            zero = jnp.zeros((group, LANES), f32)

            def some(k, carry):
                at = pl.ds(pl.multiple_of(k * group, group), group)
                his, los = zip(*(split(pairs_ref[i, at, :]) for i in range(2)))
                one, two = gather_rows(vel, 3, 0, own - 2 * rim, 2 * rim, his, los, [[zero] * 3, [zero] * 3])
                for c in range(3):
                    part[c, at, :] = one[c]
                    part[3 + c, at, :] = two[c]
                return carry

            lax.fori_loop(0, blocks // group, some, 0)

        (part,) = call(
            inner, [(6,) + slots], both, vf, pairs,
            scratch=[pltpu.VMEM((3, own - 2 * rim, LANES), f32)],
        )

        def outer(part_ref, low_ref, high_ref, got_ref, vf_ref, rims_ref, pairs_ref, trig_ref, act_ref,
                  bias_ref, fric_ref, scaled_ref, old_ref, rowsel_ref, rhs_ref, lam_ref, total, vel, lhs, stage):
            for c in range(3):
                lows = low_ref[c] + got_ref[0, c]
                highs = high_ref[c] + got_ref[1, c]
                vel[c, :rim] = rims_ref[c, :rim] + rims_ref[3, :rim] * lows[:rim]
                vel[c, rim : 2 * rim] = vf_ref[c, :rim] + vf_ref[3, :rim] * lows[rim:]
                vel[c, 2 * rim : 3 * rim] = vf_ref[c, own - rim :] + vf_ref[3, own - rim :] * highs[:rim]
                vel[c, 3 * rim :] = rims_ref[c, rim:] + rims_ref[3, rim:] * highs[rim:]
            prod = None
            for k in range(blocks // group):
                at = slice(group * k, group * (k + 1))
                sums = [[part_ref[c, at, :] for c in range(3)], [part_ref[3 + c, at, :] for c in range(3)]]
                his, los = zip(*(split(pairs_ref[i, at, :]) for i in range(2)))
                skip = own - 2 * rim
                sums = gather_rows(vel, 3, rim, rim, 0, his, los, sums)
                sums = gather_rows(vel, 3, 2 * rim, rim, skip, his, los, sums)
                one, two = sums
                (two,) = gather_rows(vel, 3, 0, rim, 0, his[1:], los[1:], [two])
                (two,) = gather_rows(vel, 3, 3 * rim, rim, skip, his[1:], los[1:], [two])
                rel = [one[c] - two[c] for c in range(3)]
                fresh, force = update(
                    [old_ref[c, at, :] for c in range(3)], rel, [trig_ref[i, at, :] for i in range(4)],
                    scaled_ref[at, :], bias_ref[at, :], fric_ref[at, :], act_ref[at, :],
                )
                for c in range(3):
                    lam_ref[c, at, :] = fresh[c]
                more = scatter_group(group * k, group, force, stage, rowsel_ref, rhs_ref, lhs, half)
                prod = more if prod is None else prod + more
            write_total(prod, total, half)

        lam, total = call(
            outer,
            [(3,) + slots, (3, rows, LANES)],
            part, low, high, got, vf, rims, pairs, trig, act, bias, friction, scaled, lam, rowsel, rhs,
            scratch=[pltpu.VMEM((3, 4 * rim, LANES), f32)] + scatter_scratch,
            onchip=[sweep < ITERS - 1, True],
        )

    both = lax.all_gather(total, "cell")
    (mine,) = call(edges(rim), [(3, rim, LANES)], both, core, specs=[VM, SM])
    got = around(mine)

    def finish(both_ref, got_ref, vf_ref, out):
        for c in range(3):
            t = both_ref[0, c, rim : rim + own] + both_ref[1, c, rim : rim + own]
            head = t[:rim] + got_ref[0, c]
            tail = t[own - rim :] + got_ref[1, c]
            v = vf_ref[c] + vf_ref[3] * jnp.concatenate([head, t[rim : own - rim], tail], axis=0)
            for r in range(own):
                out[c : c + 1, r * LANES : (r + 1) * LANES] = v[r : r + 1]

    (velocity,) = call(finish, [(3, width)], both, got, vf, onchip=[False])
    return (velocity, lam)


def solution(mesh):
    return jax.shard_map(
        on_device,
        mesh=mesh,
        in_specs=(
            P(None, "grp"),
            P("grp"),
            P(None, ("cell", "grp"), None),
            P(None, ("cell", "grp"), None),
            P(("cell", "grp"), None),
            P(("cell", "grp"), None),
            P(("cell", "grp")),
        ),
        out_specs=(P(None, "grp"), P(None, ("cell", "grp"), None)),
        check_vma=False,
    )
```
